512 devices in a mesh: space: 64 (over y, x, z_hi), chan: 8 (over z_lo, core).
Axes of the slice: x: 4, y: 8, z: 8 (z_hi: 2, z_lo: 4; z = z_hi * 4 + z_lo), core: 2. Of those that a mesh axis runs over, the one named last changes fastest.
Arguments:
- source: bfloat16 [512, 192, 128], P('chan', 'space'), may hold values from -6 to 6
- kernel: bfloat16 [7, 7, 512, 512], P(None, None, 'chan'), may hold values from -0.0390625 to 0.0390625
Outputs:
- image: bfloat16 [512, 192, 128], P('chan', 'space')
The draws below stay inside these ranges and needn't reach their ends.
All inputs are finite; a program needn't handle non-finite values.
Results may differ from the reference program's by a relative error of at most 0.001.
Values may be sent and summed in bfloat16 or wider, within the bound.
A program may use at most 64 MiB of HBM per device.

```python
import jax
import jax.numpy as jnp
from jax import lax

CH = 512
OFF = 7
NY = 128
NX = 192


def shard_levels(own_key, shape, pieces, low, high):
    gain = 1.0
    for dim, shards_of in pieces:
        heights = jax.random.uniform(jax.random.fold_in(jax.random.fold_in(own_key, 6), dim), (shards_of,), jnp.float32, low / len(pieces), high / len(pieces))
        gain = gain * jnp.repeat(jnp.exp(heights), shape[dim] // shards_of).reshape((-1,) + (1,) * (len(shape) - 1 - dim))
    return gain


def bell_draw(own_key, shape, deviation, most, split=(), kind=jnp.bfloat16):
    entries = jax.random.normal(own_key, shape, jnp.float32) * deviation
    if len(split) > 0:
        entries = shard_levels(own_key, shape, split, -0.22, 0.18) * entries
    return jnp.clip(entries, min=-most, max=most).astype(kind)


def setup_inputs(seed: int = 0) -> dict:
    streams_of = jax.random.split(jax.random.key(seed), 3)
    return {
        "source": bell_draw(streams_of[0], (CH, NX, NY), 1.0, 6.0, ((0, 8), (1, 64))),
        "kernel": bell_draw(streams_of[1], (OFF, OFF, CH, CH), (OFF * OFF * CH) ** -0.5, 0.0390625, ((2, 8),)),
    }


def reference(source, kernel):
    reach = (OFF - 1) // 2
    values = source.astype(jnp.float32)
    padded = jnp.pad(values, ((0, 0), (reach, reach), (reach, reach)))
    total = jnp.zeros(values.shape, jnp.float32)
    for row_shift in range(OFF):
        stacked = jnp.stack([padded[:, row_shift:row_shift + NX, col_shift:col_shift + NY] for col_shift in range(OFF)])
        blocks = kernel[row_shift].astype(jnp.float32)
        total = total + jnp.einsum("boc,bcxy->oxy", blocks, stacked, precision=lax.Precision.HIGHEST)
    return (values - total).astype(jnp.bfloat16)
```

```python
import functools

import jax
import jax.numpy as jnp
from jax import lax
from jax.experimental import pallas as pl
from jax.experimental.pallas import tpu as pltpu
from jax.sharding import PartitionSpec as P

OFF = 7
REACH = 3
MESH = pl.DeviceIdType.MESH


def body(rings, src, weights, out, cells, held, acc, load_sem, ring_send, ring_recv, pair_send, pair_recv, side_send, side_recv):
    space, chan = lax.axis_index("space"), lax.axis_index("chan")
    ring, half = space // 2, space % 2
    low, core = chan // 2, chan % 2
    z = half * 4 + low

    def on_ring(step):
        other = (z + step + 8) % 8
        return (ring * 2 + other // 4, (other % 4) * 2 + core)

    sibling = (space, low * 2 + 1 - core)
    forward = 1 - 2 * half
    target = (((ring + forward + rings) % rings) * 2 + half, chan)
    source = (((ring - forward + rings) % rings) * 2 + half, chan)

    load = pltpu.make_async_copy(weights, held, load_sem.at[0])
    load.start()
    mine = pltpu.make_async_copy(src, cells.at[z * 2 + core], load_sem.at[1])
    mine.start()

    barrier = pltpu.get_barrier_semaphore()
    for other in (on_ring(1), on_ring(-1), sibling, source):
        pl.semaphore_signal(barrier, inc=1, device_id=other, device_id_type=MESH)
    pl.semaphore_wait(barrier, 4)

    def slot(step):
        return ((z + step + 8) % 8) * 2 + core

    def part(ref, piece):
        return ref if piece is None else ref.at[:, pl.ds(piece * 32, 32)]

    def hop(direction, step, piece=None):
        index = slot(-direction * (step - 1))
        number = (step - 1) * 2 + (direction < 0)
        return pltpu.make_async_remote_copy(
            src_ref=part(src if step == 1 else cells.at[index], piece),
            dst_ref=part(cells.at[index], piece),
            send_sem=ring_send.at[number],
            recv_sem=ring_recv.at[number],
            device_id=on_ring(direction),
            device_id_type=MESH,
        )

    def arrived(direction, step, piece=None):
        index = slot(-direction * step)
        number = (step - 1) * 2 + (direction < 0)
        view = part(cells.at[index], piece)
        pltpu.make_async_copy(view, view, ring_recv.at[number]).wait()

    def across(index, number, from_src=False):
        return pltpu.make_async_remote_copy(
            src_ref=src if from_src else cells.at[index],
            dst_ref=cells.at[index],
            send_sem=pair_send.at[number],
            recv_sem=pair_recv.at[number],
            device_id=sibling,
            device_id_type=MESH,
        )

    def sideways(index, number):
        return pltpu.make_async_remote_copy(
            src_ref=cells.at[index],
            dst_ref=cells.at[16 + index % 8],
            send_sem=side_send.at[number],
            recv_sem=side_recv.at[number],
            device_id=target,
            device_id_type=MESH,
        )

    steps = ((1, 1), (-1, 1), (1, 2), (-1, 2), (1, 3), (-1, 3))
    hop(1, 1).start()
    hop(-1, 1).start()
    across(slot(0), 0, True).start()

    def foreign(direction, step):
        return low < step if direction > 0 else low + step > 3

    def side_arrived(direction, step, number):
        index = 16 + slot(-direction * step) % 8
        pltpu.make_async_copy(cells.at[index], cells.at[index], side_recv.at[number]).wait()
        across(index, 8 + number).start()

    for number, (direction, step) in enumerate(steps):
        arrived(direction, step)
        if step < 3:
            hop(direction, step + 1).start()
        else:
            hop(direction, 4, 0 if direction > 0 else 1).start()
        across(slot(-direction * step), 1 + number).start()

        @pl.when(foreign(direction, step))
        def _():
            sideways(slot(-direction * step), number).start()

    arrived(1, 4, 0)
    arrived(-1, 4, 1)
    sideways(slot(4), 6).start()
    across(slot(4), 7).start()
    for number, (direction, step) in enumerate(steps):

        @pl.when(foreign(direction, step))
        def _():
            side_arrived(direction, step, number)

    side_arrived(1, 4, 6)

    for number, offset in enumerate((0, -1, 1, -2, 2, -3, 3, 4)):
        index = ((z + offset + 8) % 8) * 2 + 1 - core
        pltpu.make_async_copy(cells.at[index], cells.at[index], pair_recv.at[number]).wait()
        if offset == 4:
            index = 16 + index % 8
            pltpu.make_async_copy(cells.at[index], cells.at[index], pair_recv.at[14]).wait()
        elif offset != 0:
            direction = 1 if offset < 0 else -1

            @pl.when(foreign(direction, abs(offset)))
            def _():
                side = 16 + index % 8
                pltpu.make_async_copy(cells.at[side], cells.at[side], pair_recv.at[7 + number]).wait()

    for number, (direction, step) in enumerate(steps):
        hop(direction, step).wait_send()
        across(slot(-direction * step), 1 + number).wait_send()

        @pl.when(foreign(direction, step))
        def _():
            sideways(slot(-direction * step), number).wait_send()
            across(16 + slot(-direction * step) % 8, 8 + number).wait_send()

    hop(1, 4, 0).wait_send()
    hop(-1, 4, 1).wait_send()
    across(slot(0), 0, True).wait_send()
    across(slot(4), 7).wait_send()
    sideways(slot(4), 6).wait_send()
    across(16 + slot(4) % 8, 14).wait_send()
    mine.wait()
    load.wait()

    @pl.when(jnp.logical_or(space == 0, space == rings * 2 - 1))
    def _():
        cells[pl.ds(16, 8)] = jnp.zeros((8, 3, 64, 128), jnp.bfloat16)

    bases = ((1 - half) * 16, half * 8, 8 + half * 8)
    rows = [cells[pl.ds(bases[r // 3], 8), r % 3].reshape(512, 128) for r in range(9)]
    for a in range(OFF):
        stacked = jnp.concatenate(rows[a : a + 3], axis=1)
        product = jnp.dot(held[a], stacked, preferred_element_type=jnp.float32)
        if a == 0:
            acc[...] = product
        else:
            acc[...] += product

    column = lax.broadcasted_iota(jnp.int32, (64, 128), 1)
    for i in range(3):
        total = acc[REACH * 64 : REACH * 64 + 64, i * 128 : i * 128 + 128]
        for b in range(OFF):
            if b != REACH:
                shift = b - REACH
                turned = pltpu.roll(acc[b * 64 : b * 64 + 64, i * 128 : i * 128 + 128], (-shift) % 128, 1)
                valid = column < 128 - shift if shift > 0 else column >= -shift
                total += jnp.where(valid, turned, 0.0)
        own = cells[z * 2 + core, i].astype(jnp.float32)
        out[i] = (own - total).astype(jnp.bfloat16)


def solution(mesh):
    rings = mesh.shape["space"] // 2

    def shards(source, kernel):
        rows = jnp.transpose(source, (1, 0, 2))
        weights = kernel.reshape(OFF, OFF * 64, 512)
        image = pl.pallas_call(
            functools.partial(body, rings),
            out_shape=jax.ShapeDtypeStruct(rows.shape, jnp.bfloat16),
            in_specs=[pl.BlockSpec(memory_space=pl.ANY)] * 2,
            out_specs=pl.BlockSpec(memory_space=pltpu.VMEM),
            scratch_shapes=[
                pltpu.VMEM((24, 3, 64, 128), jnp.bfloat16),
                pltpu.VMEM(weights.shape, jnp.bfloat16),
                pltpu.VMEM((OFF * 64, 384), jnp.float32),
                pltpu.SemaphoreType.DMA((2,)),
                pltpu.SemaphoreType.DMA((8,)),
                pltpu.SemaphoreType.DMA((8,)),
                pltpu.SemaphoreType.DMA((15,)),
                pltpu.SemaphoreType.DMA((15,)),
                pltpu.SemaphoreType.DMA((7,)),
                pltpu.SemaphoreType.DMA((7,)),
            ],
            compiler_params=pltpu.CompilerParams(
                collective_id=0, has_side_effects=True, vmem_limit_bytes=56 * 1024 * 1024
            ),
        )(rows, weights)
        return jnp.transpose(image, (1, 0, 2))

    placed = (P("chan", "space", None), P(None, None, "chan", None))
    return jax.shard_map(
        shards, mesh=mesh, in_specs=placed, out_specs=P("chan", "space", None), check_vma=False
    )
```
